32 devices in a mesh: blk: 4 (over y, core), grid: 8 (over z, x).
Axes of the slice: x: 2, y: 2, z: 4, core: 2. Of those that a mesh axis runs over, the one named last changes fastest.
Arguments:
- constraints: float32 [16384, 1024], P(('blk', 'grid')), may hold values from -0.1875 to 0.1875
- times_x: float32 [16384, 1024], P(('blk', 'grid')), may hold values from -6 to 6
- times_zinv: float32 [16384, 1024], P(('blk', 'grid')), may hold values from -6 to 6
- owner: int32 [4, 8, 8], P('blk', 'grid'), may hold values from 0 to 7, each once within a row
- update: float32 [4, 8, 8, 64, 1024], P('blk', 'grid'), may hold values from -6 to 6
Outputs:
- owned: float32 [4, 8, 8, 64, 1024], P('blk', 'grid')
The draws below stay inside these ranges and needn't reach their ends.
Inputs may be any that keep to these rules, and one draw needn't show every extreme that they name: Each owner[b, g, :] is a permutation of 0 to 7.
All inputs are finite; a program needn't handle non-finite values.
Results may differ from the reference program's by a relative error of at most 0.0003.
Values sent between devices are 32-bit elements; how exact they have to be, the bound alone decides.
No kernel may reach another device: no remote copies, remote signals or barrier semaphores. Data moves between devices by JAX's collectives and lax.ppermute only.
A program may use at most 64 MiB of HBM per device.

```python
import jax
import jax.numpy as jnp
from jax import lax

N = 1024
ROWS = 512
ROUNDS = 2
TILE = 64
M = 16384
N_BLK = 4
N_GRID = 8


def steps_of(own_key, shape, shards, smallest, top_value):
    def one(dim, parts):
        steps = jax.random.uniform(jax.random.fold_in(jax.random.fold_in(own_key, 6), dim), (parts,), jnp.float32, smallest / len(shards), top_value / len(shards))
        return jnp.repeat(jnp.exp(steps), shape[dim] // parts).reshape((-1,) + (1,) * (len(shape) - dim - 1))

    factor_of = one(*shards[0])
    for cut in shards[1:]:
        factor_of = factor_of * one(*cut)
    return factor_of


def noise(stream_key, extent, scale, bound, split=(), kind=jnp.bfloat16):
    values = scale * jax.random.normal(stream_key, extent, jnp.float32)
    if split:
        values = values * steps_of(stream_key, extent, split, -0.22, 0.18)
    return jnp.clip(values, -bound, bound).astype(kind)


def setup_inputs(seed: int = 0) -> dict:
    seeds = jax.random.split(jax.random.key(seed), 6)
    constraints = noise(seeds[0], (M, N), N ** -0.5, 0.1875, ((0, 32),), jnp.float32)
    times_x = noise(seeds[1], (M, N), 1.0, 6.0, ((0, 32),), jnp.float32)
    times_zinv = noise(seeds[2], (M, N), 1.0, 6.0, ((0, 32),), jnp.float32)
    owner = jax.vmap(lambda own: jax.random.permutation(own, N_GRID))(jax.random.split(seeds[3], N_BLK * N_GRID)).reshape((N_BLK, N_GRID, N_GRID)).astype(jnp.int32)
    update = noise(seeds[4], (N_BLK, N_GRID, N_GRID, TILE, ROUNDS * ROWS), 1.0, 6.0, ((0, 4), (1, 8)), jnp.float32)
    return {"constraints": constraints, "times_x": times_x, "times_zinv": times_zinv, "owner": owner, "update": update}


def reference(constraints, times_x, times_zinv, owner, update):
    blocks = N_BLK * N_GRID
    tile_rows = ROWS // N_GRID
    a_blocks = constraints.reshape(blocks, ROWS, N)
    x_blocks = times_x.reshape(blocks, ROWS, N)
    z_blocks = times_zinv.reshape(blocks, ROWS, N)

    def one_block(index):
        brow = index // N_GRID
        gcol = index % N_GRID
        rows_x = lax.dynamic_index_in_dim(x_blocks, index, 0, keepdims=False)
        rows_z = lax.dynamic_index_in_dim(z_blocks, index, 0, keepdims=False)
        columns = []
        for step in range(ROUNDS):
            source = (((brow - step) % N_BLK) * N_GRID + gcol).astype(jnp.int32)
            panel = lax.dynamic_index_in_dim(a_blocks, source, 0, keepdims=False)
            left = jnp.dot(rows_x, panel.T, preferred_element_type=jnp.float32, precision=lax.Precision.HIGHEST)
            right = jnp.dot(rows_z, panel.T, preferred_element_type=jnp.float32, precision=lax.Precision.HIGHEST)
            columns.append(left * right)
        return jnp.concatenate(columns, axis=1)

    schur = lax.map(one_block, jnp.arange(blocks, dtype=jnp.int32))
    tiles = schur.reshape(N_BLK, N_GRID, N_GRID, tile_rows, ROUNDS * ROWS)
    places = jnp.arange(N_GRID, dtype=jnp.int32)
    onehot = owner[:, :, None, :] == places[None, None, :, None]
    inverse = jnp.sum(jnp.where(onehot, places[None, None, None, :], 0), axis=3).astype(jnp.int32)
    picked = jnp.take_along_axis(tiles, inverse[:, :, :, None, None], axis=2)
    return jnp.transpose(picked, (0, 2, 1, 3, 4)) - update
```

```python
import functools

import jax
import jax.numpy as jnp
from jax import lax
from jax.experimental import pallas as pl
from jax.experimental.pallas import tpu as pltpu
from jax.sharding import PartitionSpec as P

ROUNDS = 2
HALVES = 2
NT = (((1,), (1,)), ((), ()))
ANY = pl.BlockSpec(memory_space=pl.ANY)
SMEM = pl.BlockSpec(memory_space=pltpu.SMEM)
VMEM = pl.BlockSpec(memory_space=pltpu.VMEM)


def partner(me, j, groups):
    if groups & (groups - 1) == 0:
        return me ^ j
    return lax.rem(me + j, groups)


def exchange(piece, j, groups):
    if j == 0:
        return piece
    if groups & (groups - 1) == 0:
        pairs = [(i, i ^ j) for i in range(groups)]
    else:
        pairs = [(i, (i + j) % groups) for i in range(groups)]
    return lax.ppermute(piece, "grid", pairs)


def source(me, j, groups):
    if groups & (groups - 1) == 0:
        return me ^ j
    return lax.rem(me + groups - j, groups)


def split(x):
    high = x.astype(jnp.bfloat16)
    return high, (x - high.astype(jnp.float32)).astype(jnp.bfloat16)


def tiles_kernel(js, groups, owner, x_hbm, z_hbm, panel_hbm, *refs):
    outs, (rows, panel, row_sem, panel_sem) = refs[: len(js)], refs[len(js) :]
    tile = outs[0].shape[0]
    me = lax.axis_index("grid")
    copies = []
    fetch = pltpu.make_async_copy(panel_hbm, panel, panel_sem)
    fetch.start()
    for i, j in enumerate(js):
        to = partner(me, j, groups)
        t = jnp.int32(0)
        for k in range(groups):
            t = t + jnp.where(owner[0, 0, k] == to, k, 0)
        at = pl.ds(pl.multiple_of(t * tile, tile), tile)
        for s, hbm in enumerate((x_hbm, z_hbm)):
            place = pl.ds((s * len(js) + i) * tile, tile)
            copy = pltpu.make_async_copy(hbm.at[at], rows.at[place], row_sem.at[s, i])
            copy.start()
            copies.append(copy)
    for copy in copies:
        copy.wait()
    a_hi, a_lo = split(rows[...])
    fetch.wait()
    c_hi, c_lo = split(panel[...])
    dot = functools.partial(lax.dot_general, dimension_numbers=NT, preferred_element_type=jnp.float32)
    both = dot(a_hi, c_hi) + (dot(a_lo, c_hi) + dot(a_hi, c_lo))
    for i, out in enumerate(outs):
        left = both[i * tile : (i + 1) * tile]
        right = both[(len(js) + i) * tile : (len(js) + i + 1) * tile]
        out[...] = left * right


def tiles(js, groups, owner, times_x, times_zinv, panel):
    rows, width = times_x.shape
    tile = rows // groups
    cols = panel.shape[0]
    n = len(js)
    return pl.pallas_call(
        functools.partial(tiles_kernel, js, groups),
        out_shape=[jax.ShapeDtypeStruct((tile, cols), jnp.float32)] * n,
        in_specs=[SMEM, ANY, ANY, ANY],
        out_specs=[VMEM] * n,
        scratch_shapes=[
            pltpu.VMEM((2 * n * tile, width), jnp.float32),
            pltpu.VMEM((cols, width), jnp.float32),
            pltpu.SemaphoreType.DMA((2, n)),
            pltpu.SemaphoreType.DMA,
        ],
        compiler_params=pltpu.CompilerParams(vmem_limit_bytes=32 << 20),
        cost_estimate=pl.CostEstimate(
            flops=12 * n * tile * cols * width,
            bytes_accessed=4 * (2 * n * tile * width + cols * width + n * tile * cols),
            transcendentals=0,
        ),
        name="tiles_" + "_".join(map(str, js)),
    )(owner, times_x, times_zinv, panel)


def combine_kernel(js, groups, start, size, first, *refs):
    pieces = refs[: len(js)]
    update = refs[len(js)]
    out, u_buf, o_buf, u_sem, o_sem = refs[len(js) + (1 if first else 2) :]
    me = lax.axis_index("grid")
    loads, stores = [], []
    for i, j in enumerate(js):
        at = source(me, j, groups)
        copy = pltpu.make_async_copy(update.at[at, :, pl.ds(start, size)], u_buf.at[i], u_sem.at[i])
        copy.start()
        loads.append(copy)
    for i, j in enumerate(js):
        loads[i].wait()
        o_buf[i] = pieces[i][...] - u_buf[i]
        at = source(me, j, groups)
        copy = pltpu.make_async_copy(o_buf.at[i], out.at[at, :, pl.ds(start, size)], o_sem.at[i])
        copy.start()
        stores.append(copy)
    for copy in stores:
        copy.wait()


def combine(js, groups, start, pieces, update, out):
    tile, size = pieces[0].shape
    n = len(js)
    operands = list(pieces) + [update] + ([] if out is None else [out])
    return pl.pallas_call(
        functools.partial(combine_kernel, js, groups, start, size, out is None),
        out_shape=jax.ShapeDtypeStruct(update.shape, update.dtype),
        in_specs=[VMEM] * n + [ANY] * (len(operands) - n),
        out_specs=ANY,
        scratch_shapes=[
            pltpu.VMEM((n, tile, size), jnp.float32),
            pltpu.VMEM((n, tile, size), jnp.float32),
            pltpu.SemaphoreType.DMA((n,)),
            pltpu.SemaphoreType.DMA((n,)),
        ],
        input_output_aliases={} if out is None else {n + 1: 0},
        compiler_params=pltpu.CompilerParams(vmem_limit_bytes=16 << 20),
        cost_estimate=pl.CostEstimate(
            flops=n * tile * size, bytes_accessed=12 * n * tile * size, transcendentals=0
        ),
        name="combine",
    )(*operands)


def from_behind(array, axis, by):
    length = lax.axis_size(axis)
    return lax.ppermute(array, axis, [(i, (i + by) % length) for i in range(length)])


def body(constraints, times_x, times_zinv, owner, update):
    groups = lax.axis_size("grid")
    rows, width = times_x.shape
    update = update[0, 0]
    far = [j for j in range(groups // 2, groups)]
    near = [j for j in range(groups // 2 - 1, -1, -1)]
    pick = functools.partial(tiles, groups=groups, owner=owner, times_x=times_x, times_zinv=times_zinv)
    panel = constraints
    out = None
    start = 0
    for step in range(ROUNDS):
        if step > 0:
            panel = from_behind(panel, "blk", 1)
        sets = (far[:1], far[1:], near) if step == 0 else (far, near)
        js, pieces = [], []
        for some in sets:
            for j, piece in zip(some, pick(some, panel=panel)):
                js.append(j)
                pieces.append(exchange(piece, j, groups))
        out = combine(js, groups, start, pieces, update, out)
        start += panel.shape[0]
    return out[None, None]


def solution(mesh):
    placed = (
        P(("blk", "grid"), None),
        P(("blk", "grid"), None),
        P(("blk", "grid"), None),
        P("blk", "grid", None),
        P("blk", "grid", None, None, None),
    )
    return jax.shard_map(
        body,
        mesh=mesh,
        in_specs=placed,
        out_specs=P("blk", "grid", None, None, None),
        check_vma=False,
    )
```

```python
import functools

import jax
import jax.numpy as jnp
from jax import lax
from jax.experimental import pallas as pl
from jax.experimental.pallas import tpu as pltpu
from jax.sharding import PartitionSpec as P

PARTS = 2
NT = (((1,), (1,)), ((), ()))
HBM = pl.BlockSpec(memory_space=pltpu.HBM)
VMEM = pl.BlockSpec(memory_space=pltpu.VMEM)
F32 = jnp.float32
BF16 = jnp.bfloat16


def exchange(piece, j, groups):
    return lax.ppermute(piece, "grid", [(i, i ^ j) for i in range(groups)])


def split(x):
    high = x.astype(BF16)
    return high, (x - high.astype(F32)).astype(BF16)


def dot(a, b):
    return lax.dot_general(a, b, NT, preferred_element_type=F32)


def products(rows_hi, rows_lo, panel_hi, panel_lo):
    return dot(rows_hi, panel_hi) + (dot(rows_lo, panel_hi) + dot(rows_hi, panel_lo))


def row_copies(js, groups, owner, x_hbm, z_hbm, rows, sems, base=0):
    tile = x_hbm.shape[0] // groups
    me = lax.axis_index("grid")
    copies = []
    for i, j in enumerate(js):
        to = me ^ j
        t = jnp.int32(0)
        for k in range(groups):
            t = t + jnp.where(owner[0, 0, k] == to, k, 0)
        at = pl.ds(pl.multiple_of(t * tile, tile), tile)
        place = pl.ds((base + i) * tile, tile)
        for s, hbm in enumerate((x_hbm, z_hbm)):
            copies.append(pltpu.make_async_copy(hbm.at[at], rows.at[s, place], sems.at[s, base + i]))
    return copies


def write_pieces(pieces, start, both):
    tile, cols = pieces[0].shape[1], both.shape[1]
    count = both.shape[0] // 2
    at = 0
    for piece in pieces:
        for c in range(piece.shape[0]):
            piece[c, :, start : start + cols] = both[at : at + tile] * both[count + at : count + at + tile]
            at += tile


def first_kernel(js, groups, owner_hbm, x_hbm, z_hbm, panel_hbm, *refs):
    piece, rows, hi, lo, panel, owner, owner_sem, row_sems, panel_sems = refs
    used = piece.shape[0] * piece.shape[1]
    part = panel_hbm.shape[0] // PARTS
    fetch_owner = pltpu.make_async_copy(owner_hbm, owner, owner_sem)
    fetch_owner.start()
    spans = [slice(h * part, (h + 1) * part) for h in range(PARTS)]
    fetches = []
    for h, at in enumerate(spans):
        fetches.append(pltpu.make_async_copy(panel_hbm.at[at], panel.at[at], panel_sems.at[h]))
        fetches[h].start()
    fetch_owner.wait()
    copies = row_copies(js, groups, owner, x_hbm, z_hbm, rows, row_sems)
    for copy in copies:
        copy.start()
    for h, at in enumerate(spans):
        fetches[h].wait()
        hi[at, :], lo[at, :] = split(panel[at, :])
    ready = 2 * piece.shape[0]
    for copy in copies[:ready]:
        copy.wait()
    own_hi, own_lo = split(jnp.concatenate([rows[0, :used], rows[1, :used]], axis=0))
    write_pieces([piece], 0, products(own_hi, own_lo, hi[...], lo[...]))
    for copy in copies[ready:]:
        copy.wait()


def first(js, count, groups, owner, times_x, times_zinv, panel):
    rows, width = times_x.shape
    tile, cols, n = rows // groups, panel.shape[0], len(js)
    shape = jax.ShapeDtypeStruct
    return pl.pallas_call(
        functools.partial(first_kernel, js, groups),
        out_shape=[
            shape((count, tile, cols), F32),
            shape((2, n * tile, width), F32),
            shape((cols, width), BF16),
            shape((cols, width), BF16),
        ],
        in_specs=[HBM] * 4,
        out_specs=[VMEM] * 4,
        scratch_shapes=[
            pltpu.VMEM(panel.shape, F32),
            pltpu.SMEM(owner.shape, owner.dtype),
            pltpu.SemaphoreType.DMA,
            pltpu.SemaphoreType.DMA((2, n)),
            pltpu.SemaphoreType.DMA((PARTS,)),
        ],
        compiler_params=pltpu.CompilerParams(vmem_limit_bytes=24 << 20),
        cost_estimate=pl.CostEstimate(
            flops=12 * count * tile * cols * width,
            bytes_accessed=4 * (2 * n * tile * width + cols * width),
            transcendentals=0,
        ),
        name="first",
    )(owner, times_x, times_zinv, panel)


def second_kernel(skip, js, groups, n_far, owner_hbm, x_hbm, z_hbm, rows, hi, lo, *refs):
    pieces, (more_rows, owner, owner_sem, row_sems) = refs[:-4], refs[-4:]
    fetch_owner = pltpu.make_async_copy(owner_hbm, owner, owner_sem)
    fetch_owner.start()
    tile = pieces[0].shape[1]

    def far_pieces(some, at):
        at = slice(at * tile, (at + len(some)) * tile)
        own_hi, own_lo = split(jnp.concatenate([rows[0, at], rows[1, at]], axis=0))
        write_pieces(some, 0, products(own_hi, own_lo, hi[...], lo[...]))

    far_pieces(pieces[:1], skip)
    fetch_owner.wait()
    copies = row_copies(js, groups, owner, x_hbm, z_hbm, more_rows, row_sems)
    for copy in copies:
        copy.start()
    far_pieces(pieces[1:n_far], skip + 1)
    for copy in copies:
        copy.wait()
    own_hi, own_lo = split(jnp.concatenate([more_rows[0], more_rows[1]], axis=0))
    write_pieces(pieces[n_far:], 0, products(own_hi, own_lo, hi[...], lo[...]))


def second(rows, panel, skip, far_counts, near_counts, js, tile, groups, owner, times_x, times_zinv):
    width, cols, n = rows.shape[2], panel[0].shape[0], sum(far_counts + near_counts)
    shape = jax.ShapeDtypeStruct
    out_shape = [shape((c, tile, cols), F32) for c in far_counts + near_counts]
    out_shape.append(shape((2, len(js) * tile, width), F32))
    return pl.pallas_call(
        functools.partial(second_kernel, skip, js, groups, len(far_counts)),
        out_shape=out_shape,
        in_specs=[HBM] * 3 + [VMEM] * 3,
        out_specs=[VMEM] * len(out_shape),
        scratch_shapes=[
            pltpu.SMEM(owner.shape, owner.dtype),
            pltpu.SemaphoreType.DMA,
            pltpu.SemaphoreType.DMA((2, len(js))),
        ],
        compiler_params=pltpu.CompilerParams(vmem_limit_bytes=24 << 20),
        cost_estimate=pl.CostEstimate(
            flops=12 * n * tile * cols * width,
            bytes_accessed=4 * (2 * n * tile * width + cols * width),
            transcendentals=0,
        ),
        name="second",
    )(owner, times_x, times_zinv, rows, *panel)


def more_kernel(skip, rows, panel, *pieces):
    tile = pieces[0].shape[1]
    at = slice(skip * tile, (skip + sum(p.shape[0] for p in pieces)) * tile)
    own_hi, own_lo = split(jnp.concatenate([rows[0, at], rows[1, at]], axis=0))
    write_pieces(pieces, 0, products(own_hi, own_lo, *split(panel[...])))


def more(name, rows, panel, skip, counts, tile):
    width, cols, n = rows.shape[2], panel.shape[0], sum(counts)
    return pl.pallas_call(
        functools.partial(more_kernel, skip),
        out_shape=[jax.ShapeDtypeStruct((c, tile, cols), F32) for c in counts],
        in_specs=[VMEM] * 2,
        out_specs=[VMEM] * len(counts),
        compiler_params=pltpu.CompilerParams(vmem_limit_bytes=24 << 20),
        cost_estimate=pl.CostEstimate(
            flops=12 * n * tile * cols * width,
            bytes_accessed=4 * (2 * n * tile * width + cols * width),
            transcendentals=0,
        ),
        name=name,
    )(rows, panel)


def combine_kernel(places, begun, n, *refs):
    arrays, update = refs[:n], refs[n]
    out, buf, sem = refs[n + (2 if begun else 1) :]
    me = lax.axis_index("grid")
    cols = arrays[0].shape[2]
    stores = []
    for i, (j, start) in enumerate(places):
        buf[i] = arrays[i][0] - update[me ^ j, :, start : start + cols]
        at = (me ^ j, slice(None), pl.ds(start, cols))
        stores.append(pltpu.make_async_copy(buf.at[i], out.at[at], sem.at[i]))
        stores[i].start()
    for copy in stores:
        copy.wait()


def combine(arrays, places, update, out):
    n = len(arrays)
    tile = arrays[0].shape[1:]
    operands = list(arrays) + [update] + ([] if out is None else [out])
    size = n * tile[0] * tile[1]
    return pl.pallas_call(
        functools.partial(combine_kernel, tuple(places), out is not None, n),
        out_shape=jax.ShapeDtypeStruct(update.shape, update.dtype),
        in_specs=[VMEM] * (n + 1) + [HBM] * (len(operands) - n - 1),
        out_specs=HBM,
        scratch_shapes=[pltpu.VMEM((n, *tile), F32), pltpu.SemaphoreType.DMA((n,))],
        input_output_aliases={} if out is None else {n + 1: 0},
        compiler_params=pltpu.CompilerParams(vmem_limit_bytes=16 << 20),
        cost_estimate=pl.CostEstimate(flops=size, bytes_accessed=12 * size, transcendentals=0),
        name="combine",
    )(*operands)


def after(value, *earlier):
    return lax.optimization_barrier((value, *earlier))[0] if earlier else value


def from_behind(array, axis, by):
    length = lax.axis_size(axis)
    return lax.ppermute(array, axis, [(i, (i + by) % length) for i in range(length)])


def body(constraints, times_x, times_zinv, owner, update):
    groups = lax.axis_size("grid")
    tile = times_x.shape[0] // groups
    cols = constraints.shape[0]
    update = update[0, 0]
    times_x, times_zinv, panel, owner = (
        pltpu.with_memory_space_constraint(a, pltpu.HBM) for a in (times_x, times_zinv, constraints, owner)
    )
    half = groups // 2
    far = tuple(range(half, groups))
    near = (*range(2, half), 1, 0)
    ones = (1,) * half

    moved = from_behind(constraints, "blk", 1)
    piece, far_rows, *panel = first(far, 1, groups, owner, times_x, times_zinv, panel)
    *pieces, near_rows = second(
        far_rows, panel, 1, ones[1:], ones, near, tile, groups, owner, times_x, times_zinv
    )
    ready = dict(zip([(j, 0) for j in far + near], [piece, *pieces]))
    got = {}

    def send(*keys):
        for key in keys:
            got[key] = exchange(ready[key], key[0], groups) if key[0] else ready[key]

    a, a2, n, n2 = ([(j, step) for j in some] for some in (far, near[:-1]) for step in range(2))
    own, own2 = (0, 0), (0, 1)
    send(*ready)
    moved = after(moved, *[got[key] for key in a[:2] + n[:1]])
    ready.update(zip(a2[:1], more("more_first", far_rows, moved, 0, (1,), tile)))
    ready.update(zip(a2[1:], more("more_far", far_rows, moved, 1, ones[1:], tile)))
    ready.update(zip([*n2, own2], more("more_near", near_rows, moved, 0, ones, tile)))
    send(*a2, *n2, own2)
    out = None
    for keys in ([own, *a[:2], *n[:1], *a[2:], *n[1:]], [own2, *a2[:-1], *n2[:1]], [*n2[1:2], a2[-1], *n2[2:]]):
        out = combine([got[key] for key in keys], [(j, step * cols) for j, step in keys], update, out)
    return out[None, None]


def solution(mesh):
    placed = (
        P(("blk", "grid"), None),
        P(("blk", "grid"), None),
        P(("blk", "grid"), None),
        P("blk", "grid", None),
        P("blk", "grid", None, None, None),
    )
    return jax.shard_map(
        body,
        mesh=mesh,
        in_specs=placed,
        out_specs=P("blk", "grid", None, None, None),
        check_vma=False,
    )
```

```python
import functools

import jax
import jax.numpy as jnp
from jax import lax
from jax.experimental import pallas as pl
from jax.experimental.pallas import tpu as pltpu
from jax.sharding import PartitionSpec as P

PARTS = 2
NT = (((1,), (1,)), ((), ()))
HBM = pl.BlockSpec(memory_space=pltpu.HBM)
VMEM = pl.BlockSpec(memory_space=pltpu.VMEM)
F32 = jnp.float32
BF16 = jnp.bfloat16


def exchange(piece, j, groups):
    return lax.ppermute(piece, "grid", [(i, i ^ j) for i in range(groups)])


def split(x):
    high = x.astype(BF16)
    return high, (x - high.astype(F32)).astype(BF16)


def dot(a, b):
    return lax.dot_general(a, b, NT, preferred_element_type=F32)


def products(rows_hi, rows_lo, panel_hi, panel_lo):
    return dot(rows_hi, panel_hi) + (dot(rows_lo, panel_hi) + dot(rows_hi, panel_lo))


def row_copies(js, groups, owner, x_hbm, z_hbm, rows, sems, base=0):
    tile = x_hbm.shape[0] // groups
    me = lax.axis_index("grid")
    copies = []
    for i, j in enumerate(js):
        to = me ^ j
        t = jnp.int32(0)
        for k in range(groups):
            t = t + jnp.where(owner[0, 0, k] == to, k, 0)
        at = pl.ds(pl.multiple_of(t * tile, tile), tile)
        place = pl.ds((base + i) * tile, tile)
        for s, hbm in enumerate((x_hbm, z_hbm)):
            copies.append(pltpu.make_async_copy(hbm.at[at], rows.at[s, place], sems.at[s, base + i]))
    return copies


def write_pieces(pieces, start, both):
    tile, cols = pieces[0].shape[1], both.shape[1]
    count = both.shape[0] // 2
    at = 0
    for piece in pieces:
        for c in range(piece.shape[0]):
            piece[c, :, start : start + cols] = both[at : at + tile] * both[count + at : count + at + tile]
            at += tile


def first_kernel(js, groups, owner_hbm, x_hbm, z_hbm, panel_hbm, *refs):
    piece, rows, hi, lo, panel, owner, owner_sem, row_sems, panel_sems = refs
    used = piece.shape[0] * piece.shape[1]
    part = panel_hbm.shape[0] // PARTS
    fetch_owner = pltpu.make_async_copy(owner_hbm, owner, owner_sem)
    fetch_owner.start()
    spans = [slice(h * part, (h + 1) * part) for h in range(PARTS)]
    fetches = []
    for h, at in enumerate(spans):
        fetches.append(pltpu.make_async_copy(panel_hbm.at[at], panel.at[at], panel_sems.at[h]))
        fetches[h].start()
    fetch_owner.wait()
    copies = row_copies(js, groups, owner, x_hbm, z_hbm, rows, row_sems)
    for copy in copies:
        copy.start()
    for h, at in enumerate(spans):
        fetches[h].wait()
        hi[at, :], lo[at, :] = split(panel[at, :])
    ready = 2 * piece.shape[0]
    for copy in copies[:ready]:
        copy.wait()
    own_hi, own_lo = split(jnp.concatenate([rows[0, :used], rows[1, :used]], axis=0))
    write_pieces([piece], 0, products(own_hi, own_lo, hi[...], lo[...]))
    for copy in copies[ready:]:
        copy.wait()


def first(js, count, groups, owner, times_x, times_zinv, panel):
    rows, width = times_x.shape
    tile, cols, n = rows // groups, panel.shape[0], len(js)
    shape = jax.ShapeDtypeStruct
    return pl.pallas_call(
        functools.partial(first_kernel, js, groups),
        out_shape=[
            shape((count, tile, cols), F32),
            shape((2, n * tile, width), F32),
            shape((cols, width), BF16),
            shape((cols, width), BF16),
        ],
        in_specs=[HBM] * 4,
        out_specs=[VMEM] * 4,
        scratch_shapes=[
            pltpu.VMEM(panel.shape, F32),
            pltpu.SMEM(owner.shape, owner.dtype),
            pltpu.SemaphoreType.DMA,
            pltpu.SemaphoreType.DMA((2, n)),
            pltpu.SemaphoreType.DMA((PARTS,)),
        ],
        compiler_params=pltpu.CompilerParams(vmem_limit_bytes=24 << 20),
        cost_estimate=pl.CostEstimate(
            flops=12 * count * tile * cols * width,
            bytes_accessed=4 * (2 * n * tile * width + cols * width),
            transcendentals=0,
        ),
        name="first",
    )(owner, times_x, times_zinv, panel)


def second_kernel(skip, js, groups, n_far, owner_hbm, x_hbm, z_hbm, rows, hi, lo, *refs):
    pieces, (more_rows, owner, owner_sem, row_sems) = refs[:-4], refs[-4:]
    fetch_owner = pltpu.make_async_copy(owner_hbm, owner, owner_sem)
    fetch_owner.start()
    tile = pieces[0].shape[1]

    def far_pieces(some, at):
        at = slice(at * tile, (at + len(some)) * tile)
        own_hi, own_lo = split(jnp.concatenate([rows[0, at], rows[1, at]], axis=0))
        write_pieces(some, 0, products(own_hi, own_lo, hi[...], lo[...]))

    far_pieces(pieces[:1], skip)
    fetch_owner.wait()
    copies = row_copies(js, groups, owner, x_hbm, z_hbm, more_rows, row_sems)
    for copy in copies:
        copy.start()
    far_pieces(pieces[1:n_far], skip + 1)
    for copy in copies:
        copy.wait()
    own_hi, own_lo = split(jnp.concatenate([more_rows[0], more_rows[1]], axis=0))
    write_pieces(pieces[n_far:], 0, products(own_hi, own_lo, hi[...], lo[...]))


def second(rows, panel, skip, far_counts, near_counts, js, tile, groups, owner, times_x, times_zinv):
    width, cols, n = rows.shape[2], panel[0].shape[0], sum(far_counts + near_counts)
    shape = jax.ShapeDtypeStruct
    out_shape = [shape((c, tile, cols), F32) for c in far_counts + near_counts]
    out_shape.append(shape((2, len(js) * tile, width), F32))
    return pl.pallas_call(
        functools.partial(second_kernel, skip, js, groups, len(far_counts)),
        out_shape=out_shape,
        in_specs=[HBM] * 3 + [VMEM] * 3,
        out_specs=[VMEM] * len(out_shape),
        scratch_shapes=[
            pltpu.SMEM(owner.shape, owner.dtype),
            pltpu.SemaphoreType.DMA,
            pltpu.SemaphoreType.DMA((2, len(js))),
        ],
        compiler_params=pltpu.CompilerParams(vmem_limit_bytes=24 << 20),
        cost_estimate=pl.CostEstimate(
            flops=12 * n * tile * cols * width,
            bytes_accessed=4 * (2 * n * tile * width + cols * width),
            transcendentals=0,
        ),
        name="second",
    )(owner, times_x, times_zinv, rows, *panel)


def more_kernel(skip, rows, panel, *pieces):
    tile = pieces[0].shape[1]
    at = slice(skip * tile, (skip + sum(p.shape[0] for p in pieces)) * tile)
    own_hi, own_lo = split(jnp.concatenate([rows[0, at], rows[1, at]], axis=0))
    write_pieces(pieces, 0, products(own_hi, own_lo, *split(panel[...])))


def more(name, rows, panel, skip, counts, tile):
    width, cols, n = rows.shape[2], panel.shape[0], sum(counts)
    return pl.pallas_call(
        functools.partial(more_kernel, skip),
        out_shape=[jax.ShapeDtypeStruct((c, tile, cols), F32) for c in counts],
        in_specs=[VMEM] * 2,
        out_specs=[VMEM] * len(counts),
        compiler_params=pltpu.CompilerParams(vmem_limit_bytes=24 << 20),
        cost_estimate=pl.CostEstimate(
            flops=12 * n * tile * cols * width,
            bytes_accessed=4 * (2 * n * tile * width + cols * width),
            transcendentals=0,
        ),
        name=name,
    )(rows, panel)


def combine_kernel(places, begun, n, *refs):
    arrays, update = refs[:n], refs[n]
    out, buf, sem = refs[n + (2 if begun else 1) :]
    me = lax.axis_index("grid")
    cols = arrays[0].shape[2]
    stores = []
    for i, (j, start) in enumerate(places):
        buf[i] = arrays[i][0] - update[me ^ j, :, start : start + cols]
        at = (me ^ j, slice(None), pl.ds(start, cols))
        stores.append(pltpu.make_async_copy(buf.at[i], out.at[at], sem.at[i]))
        stores[i].start()
    for copy in stores:
        copy.wait()


def combine(arrays, places, update, out):
    n = len(arrays)
    tile = arrays[0].shape[1:]
    operands = list(arrays) + [update] + ([] if out is None else [out])
    size = n * tile[0] * tile[1]
    return pl.pallas_call(
        functools.partial(combine_kernel, tuple(places), out is not None, n),
        out_shape=jax.ShapeDtypeStruct(update.shape, update.dtype),
        in_specs=[VMEM] * (n + 1) + [HBM] * (len(operands) - n - 1),
        out_specs=HBM,
        scratch_shapes=[pltpu.VMEM((n, *tile), F32), pltpu.SemaphoreType.DMA((n,))],
        input_output_aliases={} if out is None else {n + 1: 0},
        compiler_params=pltpu.CompilerParams(vmem_limit_bytes=16 << 20),
        cost_estimate=pl.CostEstimate(flops=size, bytes_accessed=12 * size, transcendentals=0),
        name="combine",
    )(*operands)


def after(value, *earlier):
    return lax.optimization_barrier((value, *earlier))[0] if earlier else value


def from_behind(array, axis, by):
    length = lax.axis_size(axis)
    return lax.ppermute(array, axis, [(i, (i + by) % length) for i in range(length)])


def body(constraints, times_x, times_zinv, owner, update):
    groups = lax.axis_size("grid")
    tile = times_x.shape[0] // groups
    cols = constraints.shape[0]
    update = update[0, 0]
    times_x, times_zinv, panel, owner = (
        pltpu.with_memory_space_constraint(a, pltpu.HBM) for a in (times_x, times_zinv, constraints, owner)
    )
    half = groups // 2
    far = tuple(range(half, groups))
    near = (*range(2, half), 1, 0)
    ones = (1,) * half

    moved = from_behind(constraints, "blk", 1)
    piece, far_rows, *panel = first(far, 1, groups, owner, times_x, times_zinv, panel)
    *pieces, near_rows = second(
        far_rows, panel, 1, ones[1:], ones, near, tile, groups, owner, times_x, times_zinv
    )
    ready = dict(zip([(j, 0) for j in far + near], [piece, *pieces]))
    got = {}

    def send(*keys):
        for key in keys:
            got[key] = exchange(ready[key], key[0], groups) if key[0] else ready[key]

    a, a2, n, n2 = ([(j, step) for j in some] for some in (far, (*range(half - 1, 1, -1), 1)) for step in range(2))
    own, own2 = (0, 0), (0, 1)
    send(*ready)
    moved = after(moved, *[got[key] for key in a[:2] + n[:1]])
    ready.update(zip(a2[:1], more("more_first", far_rows, moved, 0, (1,), tile)))
    ready.update(zip(a2[1:], more("more_far", far_rows, moved, 1, ones[1:], tile)))
    ready.update(zip([(j, 1) for j in near], more("more_near", near_rows, moved, 0, ones, tile)))
    send(*a2, *n2, own2)
    out = None
    plan = (
        [own, *a[:2], *n[:1], *a[2:], *n[1:]],
        [own2, *a2[:-1], *n2[-1:]],
        [*n2[:1], a2[-1], *n2[1:-1]],
    )
    for keys in plan:
        out = combine([got[key] for key in keys], [(j, step * cols) for j, step in keys], update, out)
    return out[None, None]


def solution(mesh):
    placed = (
        P(("blk", "grid"), None),
        P(("blk", "grid"), None),
        P(("blk", "grid"), None),
        P("blk", "grid", None),
        P("blk", "grid", None, None, None),
    )
    return jax.shard_map(
        body,
        mesh=mesh,
        in_specs=placed,
        out_specs=P("blk", "grid", None, None, None),
        check_vma=False,
    )
```
